32 devices in a mesh: sky: 2 (over x), tm: 16 (over z, y, core).
Axes of the slice: x: 2, y: 2, z: 4, core: 2. Of those that a mesh axis runs over, the one named last changes fastest.
Arguments:
- series: bfloat16 [4, 4, 1024, 2048], P('sky', None, 'tm'), parts along dimension 0, may hold values from -6 to 6
- antenna: float32 [4, 3], P('sky'), parts along dimension 0, as said below
- offsets: int32 [16, 2], P('sky'), parts along dimension 0, may hold values from -8 to 8, as said below
Outputs:
- detection: float32 [16, 1024, 2048], P('sky', 'tm'), parts along dimension 0
The draws below stay inside these ranges and needn't reach their ends.
There are 2 independent parts, one for each index of `sky`. The reference program is written for one: setup_inputs(seed, part) draws one part's arguments, and reference() takes and returns one part's arrays. A program takes and returns all parts, laid end to end along the dimension named above; each array names one. Nothing has to cross between parts.
Inputs may be any that keep to these rules, and one draw needn't show every extreme that they name: `offsets`: both -8 and 8 occur in every draw. `antenna`: A and B are positive and C C is at most 0.49 A B in every row.
All inputs are finite; a program needn't handle non-finite values.
Results may differ from the reference program's by a relative error of at most 0.0032.
Values may be sent and summed in bfloat16 or wider, within the bound.
A program may use at most 128 MiB of HBM per device.

```python
import math
import jax
import jax.numpy as jnp
from jax import lax

NA = 2048
NB = 1024
LEN = 2097152
SEG = 2
TEMPL = 8
DMAX = 8


def draw_antenna(key, part):
    key_a, key_b, key_c = jax.random.split(key, 3)
    coef_a = jnp.exp(jax.random.uniform(key_a, (SEG,), jnp.float32, math.log(0.5), math.log(2.0)))
    coef_b = jnp.exp(jax.random.uniform(key_b, (SEG,), jnp.float32, math.log(0.5), math.log(2.0)))
    mixing = jax.random.uniform(key_c, (SEG,), jnp.float32, -1.0, 1.0)
    coef_c = 0.7 * mixing * jnp.sqrt(coef_a * coef_b)
    return jnp.stack([coef_a, coef_b, coef_c], axis=1).astype(jnp.float32)


def draw_offsets(key, part):
    drawn = jax.random.randint(key, (TEMPL, SEG), -DMAX, DMAX + 1, dtype=jnp.int32)
    drawn = drawn.at[0, 0].set(DMAX)
    drawn = drawn.at[1, 0].set(-DMAX)
    return drawn.astype(jnp.int32)


def block_scale(stream_key, shape, cuts, smallest, top_value):
    gain = 1.0
    for axis_at, blocks in cuts:
        draws = jax.random.uniform(jax.random.fold_in(jax.random.fold_in(stream_key, 6), axis_at), (blocks,), jnp.float32, smallest / len(cuts), top_value / len(cuts))
        gain = gain * jnp.repeat(jnp.exp(draws), shape[axis_at] // blocks).reshape((-1,) + (1,) * (len(shape) - 1 - axis_at))
    return gain


def bell_draw(key, shape, width, most, cuts=(), kind=jnp.bfloat16):
    gain = block_scale(key, shape, cuts, -0.22, 0.18) if cuts else 1.0
    values = jax.random.normal(key, shape, jnp.float32) * width * gain
    return jnp.minimum(jnp.maximum(values, -most), most).astype(kind)


def setup_inputs(seed: int = 0, part: int = 0) -> dict:
    seeds = jax.random.split(jax.random.key(seed), 4)
    part_splits = jax.random.split(jax.random.fold_in(seeds[3], part), 4)
    return {
        "series": bell_draw(part_splits[0], (SEG, 4, NB, NA), 1.0, 6.0, ((2, 16),)),
        "antenna": draw_antenna(jax.random.fold_in(jax.random.fold_in(seeds[3], part), 71), part),
        "offsets": draw_offsets(jax.random.fold_in(jax.random.fold_in(seeds[3], part), 71), part),
    }


def dft_table(length):
    indices = jnp.arange(length, dtype=jnp.int32)
    products = (indices[:, None] * indices[None, :]) % length
    phase_angle = products.astype(jnp.float32) * (2.0 * math.pi / length)
    return jnp.cos(phase_angle).astype(jnp.bfloat16), (-jnp.sin(phase_angle)).astype(jnp.bfloat16)


def complex_dft(x_real, x_imag, w_real, w_imag, formula):
    x_real = x_real.astype(jnp.float32)
    x_imag = x_imag.astype(jnp.float32)
    w_real = w_real.astype(jnp.float32)
    w_imag = w_imag.astype(jnp.float32)
    real_part = jnp.einsum(formula, x_real, w_real) - jnp.einsum(formula, x_imag, w_imag)
    imag_part = jnp.einsum(formula, x_real, w_imag) + jnp.einsum(formula, x_imag, w_real)
    return real_part, imag_part


def projection(spectra, antenna):
    coef_a = antenna[:, 0][:, None, None]
    coef_b = antenna[:, 1][:, None, None]
    coef_c = antenna[:, 2][:, None, None]
    a_real, a_imag, b_real, b_imag = spectra[:, 0], spectra[:, 1], spectra[:, 2], spectra[:, 3]
    numer = coef_b * (a_real * a_real + a_imag * a_imag) + coef_a * (b_real * b_real + b_imag * b_imag) - 2.0 * coef_c * (a_real * b_real + a_imag * b_imag)
    return numer / ((coef_a * coef_b - coef_c * coef_c) * LEN)


def reference(series, antenna, offsets):
    short_real, short_imag = dft_table(NB)
    long_real, long_imag = dft_table(NA)
    columns = jnp.arange(NA, dtype=jnp.int32)
    bins = jnp.arange(NB, dtype=jnp.int32)
    twist = ((columns[:, None] * bins[None, :]) % LEN).astype(jnp.float32) * (2.0 * math.pi / LEN)
    twid_real = jnp.cos(twist)
    twid_imag = -jnp.sin(twist)
    comps = []
    for lead in (0, 2):
        real_part, imag_part = complex_dft(series[:, lead], series[:, lead + 1], short_real, short_imag, "snj,nk->sjk")
        turned_real = (real_part * twid_real - imag_part * twid_imag).astype(jnp.bfloat16)
        turned_imag = (real_part * twid_imag + imag_part * twid_real).astype(jnp.bfloat16)
        out_real, out_imag = complex_dft(turned_real, turned_imag, long_real, long_imag, "sjk,jm->skm")
        comps += [out_real, out_imag]
    spectra = jnp.stack(comps, axis=1)
    fstat = projection(spectra, antenna)
    spectrum_line = jnp.transpose(fstat, (0, 2, 1)).reshape(SEG, LEN)

    def one_template(shift_row):
        total_sum = jnp.zeros((LEN,), jnp.float32)
        for segment in range(SEG):
            total_sum = total_sum + jnp.roll(spectrum_line[segment], -shift_row[segment])
        return (total_sum / SEG).reshape(NA, NB).T

    return lax.map(one_template, offsets)
```

```python
import functools
import math

import jax
import jax.numpy as jnp
from jax import lax
from jax.experimental import pallas as pl
from jax.experimental.pallas import tpu as pltpu
from jax.sharding import PartitionSpec as P

DMAX = 8
LOW = 64


def unit(products, length):
    angle = products.astype(jnp.float32) * (2.0 * math.pi / length)
    return jnp.cos(angle), -jnp.sin(angle)


def dft_table(length):
    bins = jnp.arange(length, dtype=jnp.int32)[None, :]
    high = LOW * jnp.arange(length // LOW, dtype=jnp.int32)[:, None]
    low = jnp.arange(LOW, dtype=jnp.int32)[:, None]
    thin = unit(high * bins % length, length) + unit(low * bins % length, length)
    high_real, high_imag, low_real, low_imag = lax.optimization_barrier(thin)
    high_real, high_imag = high_real[:, None], high_imag[:, None]
    real = (high_real * low_real - high_imag * low_imag).astype(jnp.bfloat16)
    imag = (high_real * low_imag + high_imag * low_real).astype(jnp.bfloat16)
    return real.reshape(length, length), imag.reshape(length, length)


def dot(x, y):
    return jnp.dot(x, y, preferred_element_type=jnp.float32)


def first_kernel(x_ref, wr_ref, wi_ref, tr_ref, ti_ref, out_ref):
    width = x_ref.shape[-1]
    if width % 128 == 0:
        both = jnp.concatenate([x_ref[0, 0], x_ref[0, 1]], axis=-1)
        by_real = dot(wr_ref[...], both)
        by_imag = dot(wi_ref[...], both)
        real = by_real[:, :width] - by_imag[:, width:]
        imag = by_imag[:, :width] + by_real[:, width:]
    else:
        real = dot(wr_ref[...], x_ref[0, 0]) - dot(wi_ref[...], x_ref[0, 1])
        imag = dot(wi_ref[...], x_ref[0, 0]) + dot(wr_ref[...], x_ref[0, 1])
    tr, ti = tr_ref[...], ti_ref[...]
    out_ref[0, 0] = (real * tr - imag * ti).astype(jnp.bfloat16)
    out_ref[0, 1] = (real * ti + imag * tr).astype(jnp.bfloat16)


def first_stage(members, table, twiddle):
    segs, comps, rows, width = members.shape
    tile = min(256, rows)
    whole = pl.BlockSpec((1, 2, rows, width), lambda s, c, r: (s, c, 0, 0))
    strip = pl.BlockSpec((tile, rows), lambda s, c, r: (r, 0))
    turn = pl.BlockSpec((tile, width), lambda s, c, r: (r, 0))
    return pl.pallas_call(
        first_kernel,
        grid=(segs, comps // 2, rows // tile),
        in_specs=[whole, strip, strip, turn, turn],
        out_specs=pl.BlockSpec((1, 2, tile, width), lambda s, c, r: (s, c, r, 0)),
        out_shape=jax.ShapeDtypeStruct(members.shape, jnp.bfloat16),
    )(members, *table, *twiddle)


def second_kernel(bins, coef_ref, x_ref, wr_ref, wi_ref, out_ref):
    segs, comps, rows, length = x_ref.shape
    flat = x_ref[...].reshape(segs * comps * rows, length)
    by_real = dot(flat, wr_ref[...]).reshape(segs, comps, rows, -1)
    by_imag = dot(flat, wi_ref[...]).reshape(segs, comps, rows, -1)
    for s in range(segs):
        ar = by_real[s, 0] - by_imag[s, 1]
        ai = by_imag[s, 0] + by_real[s, 1]
        br = by_real[s, 2] - by_imag[s, 3]
        bi = by_imag[s, 2] + by_real[s, 3]
        a, b, c = coef_ref[s, 0], coef_ref[s, 1], coef_ref[s, 2]
        numer = b * (ar * ar + ai * ai) + a * (br * br + bi * bi) - 2.0 * c * (ar * br + ai * bi)
        out_ref[s] = numer / ((a * b - c * c) * bins)


def second_stage(members, table, antenna, bins):
    segs, comps, rows, length = members.shape
    tile = min(512, length)
    column = pl.BlockSpec((length, tile), lambda k: (0, k))
    return pl.pallas_call(
        functools.partial(second_kernel, float(bins)),
        grid=(length // tile,),
        in_specs=[
            pl.BlockSpec(memory_space=pltpu.SMEM),
            pl.BlockSpec(members.shape, lambda k: (0, 0, 0, 0)),
            column,
            column,
        ],
        out_specs=pl.BlockSpec((segs, rows, tile), lambda k: (0, 0, k)),
        out_shape=jax.ShapeDtypeStruct((segs, rows, length), jnp.float32),
    )(antenna, members, *table)


def shifted(wide, s, start, rows):
    part = lax.rem(start, 8)
    base = pl.multiple_of(start - part, 8)
    tiles = wide[s, pl.ds(base, rows + 8), :].reshape(rows // 8 + 1, 8, -1)
    turned = pltpu.roll(tiles, lax.rem(8 - part, 8), 1)
    here = lax.broadcasted_iota(jnp.int32, turned[1:].shape, 1) < 8 - part
    return jnp.where(here, turned[:-1], turned[1:]).reshape(rows, -1)


def detect_kernel(last, place_ref, off_ref, low_ref, mid_ref, up_ref, out_ref, wide):
    segs, rows, length = mid_ref.shape
    t = pl.program_id(0)

    @pl.when(t == 0)
    def _():
        wide[:, DMAX : DMAX + rows] = mid_ref[...]
        for s in range(segs):
            low, up = low_ref[s], up_ref[s]
            wide[s, :DMAX] = jnp.where(place_ref[0] == 0, pltpu.roll(low, 1, 1), low)
            wide[s, DMAX + rows : 2 * DMAX + rows] = jnp.where(
                place_ref[0] == last, pltpu.roll(up, length - 1, 1), up
            )

    total = shifted(wide, 0, DMAX + off_ref[t, 0], rows)
    for s in range(1, segs):
        total = total + shifted(wide, s, DMAX + off_ref[t, s], rows)
    out_ref[0] = total / segs


def detect(fstat, offsets):
    segs, rows, length = fstat.shape
    count = lax.axis_size("tm")
    lower = lax.ppermute(
        fstat[:, rows - DMAX :], "tm", [(i, (i + 1) % count) for i in range(count)]
    )
    upper = lax.ppermute(fstat[:, :DMAX], "tm", [((i + 1) % count, i) for i in range(count)])
    place = lax.axis_index("tm").reshape(1)
    templates = offsets.shape[0]
    smem = pl.BlockSpec(memory_space=pltpu.SMEM)
    rim = pl.BlockSpec((segs, DMAX, length), lambda t: (0, 0, 0))
    return pl.pallas_call(
        functools.partial(detect_kernel, count - 1),
        grid=(templates,),
        in_specs=[smem, smem, rim, pl.BlockSpec(fstat.shape, lambda t: (0, 0, 0)), rim],
        out_specs=pl.BlockSpec((1, rows, length), lambda t: (t, 0, 0)),
        out_shape=jax.ShapeDtypeStruct((templates, rows, length), jnp.float32),
        scratch_shapes=[pltpu.VMEM((segs, rows + 3 * DMAX, length), jnp.float32)],
    )(place, offsets, lower, fstat, upper)


def local(series, antenna, offsets):
    count = lax.axis_size("tm")
    rows, length = series.shape[2] * count, series.shape[3]
    width = length // count
    bins = rows * length
    columns = lax.axis_index("tm") * width + jnp.arange(width, dtype=jnp.int32)
    turns = jnp.arange(rows, dtype=jnp.int32)[:, None] * columns[None, :] % bins
    twiddle = unit(turns, bins)
    short, long = dft_table(rows), dft_table(length)
    members = lax.all_to_all(series, "tm", split_axis=3, concat_axis=2, tiled=True)
    twiddled = first_stage(members, short, twiddle)
    members = lax.all_to_all(twiddled, "tm", split_axis=2, concat_axis=3, tiled=True)
    fstat = second_stage(members, long, antenna, bins)
    return detect(fstat, offsets)


def solution(mesh):
    return jax.shard_map(
        local,
        mesh=mesh,
        in_specs=(P("sky", None, "tm", None), P("sky", None), P("sky", None)),
        out_specs=P("sky", "tm", None),
        check_vma=False,
    )
```

```python
import functools
import math

import jax
import jax.numpy as jnp
from jax import lax
from jax.experimental import pallas as pl
from jax.experimental.pallas import tpu as pltpu
from jax.sharding import PartitionSpec as P

DMAX = 8
LOW = 64


def unit(products, length):
    angle = products.astype(jnp.float32) * (2.0 * math.pi / length)
    return jnp.cos(angle), -jnp.sin(angle)


def thin_tables(length, columns, rows, low_rows):
    columns = columns[None, :]
    high = low_rows * jnp.arange(rows // low_rows, dtype=jnp.int32)[:, None]
    low = jnp.arange(low_rows, dtype=jnp.int32)[:, None]
    thin = unit(high * columns % length, length) + unit(low * columns % length, length)
    return lax.optimization_barrier(thin)


def turned_by(high_real, high_imag, low_real, low_imag):
    real = high_real * low_real - high_imag * low_imag
    imag = high_real * low_imag + high_imag * low_real
    return real, imag


def dft_table(length):
    thin = thin_tables(length, jnp.arange(length, dtype=jnp.int32), length, LOW)
    real, imag = turned_by(thin[0][:, None], thin[1][:, None], *thin[2:])
    real, imag = real.astype(jnp.bfloat16), imag.astype(jnp.bfloat16)
    return real.reshape(length, length), imag.reshape(length, length)


def dot(x, y):
    return jnp.dot(x, y, preferred_element_type=jnp.float32)


def first_kernel(x_ref, wr_ref, wi_ref, tr_ref, ti_ref, out_ref):
    width = x_ref.shape[-1]
    if width % 128 == 0:
        both = jnp.concatenate([x_ref[0, 0], x_ref[0, 1]], axis=-1)
        by_real = dot(wr_ref[...], both)
        by_imag = dot(wi_ref[...], both)
        real = by_real[:, :width] - by_imag[:, width:]
        imag = by_imag[:, :width] + by_real[:, width:]
    else:
        real = dot(wr_ref[...], x_ref[0, 0]) - dot(wi_ref[...], x_ref[0, 1])
        imag = dot(wi_ref[...], x_ref[0, 0]) + dot(wr_ref[...], x_ref[0, 1])
    tr, ti = tr_ref[...], ti_ref[...]
    out_ref[0, 0] = (real * tr - imag * ti).astype(jnp.bfloat16)
    out_ref[0, 1] = (real * ti + imag * tr).astype(jnp.bfloat16)


def first_stage(members, table, twiddle):
    segs, comps, rows, width = members.shape
    tile = min(256, rows)
    whole = pl.BlockSpec((1, 2, rows, width), lambda s, c, r: (s, c, 0, 0))
    strip = pl.BlockSpec((tile, rows), lambda s, c, r: (r, 0))
    turn = pl.BlockSpec((tile, width), lambda s, c, r: (r, 0))
    return pl.pallas_call(
        first_kernel,
        grid=(segs, comps // 2, rows // tile),
        in_specs=[whole, strip, strip, turn, turn],
        out_specs=pl.BlockSpec((1, 2, tile, width), lambda s, c, r: (s, c, r, 0)),
        out_shape=jax.ShapeDtypeStruct(members.shape, jnp.bfloat16),
    )(members, *table, *twiddle)


def second_kernel(bins, coef_ref, x_ref, wr_ref, wi_ref, out_ref):
    segs, comps, rows, length = x_ref.shape
    flat = x_ref[...].reshape(segs * comps * rows, length)
    by_real = dot(flat, wr_ref[...]).reshape(segs, comps, rows, -1)
    by_imag = dot(flat, wi_ref[...]).reshape(segs, comps, rows, -1)
    for s in range(segs):
        ar = by_real[s, 0] - by_imag[s, 1]
        ai = by_imag[s, 0] + by_real[s, 1]
        br = by_real[s, 2] - by_imag[s, 3]
        bi = by_imag[s, 2] + by_real[s, 3]
        a, b, c = coef_ref[s, 0], coef_ref[s, 1], coef_ref[s, 2]
        numer = b * (ar * ar + ai * ai) + a * (br * br + bi * bi) - 2.0 * c * (ar * br + ai * bi)
        out_ref[s] = numer / ((a * b - c * c) * bins)


def second_stage(members, table, antenna, bins):
    segs, comps, rows, length = members.shape
    tile = min(512, length)
    column = pl.BlockSpec((length, tile), lambda k: (0, k))
    return pl.pallas_call(
        functools.partial(second_kernel, float(bins)),
        grid=(length // tile,),
        in_specs=[
            pl.BlockSpec(memory_space=pltpu.SMEM),
            pl.BlockSpec(members.shape, lambda k: (0, 0, 0, 0)),
            column,
            column,
        ],
        out_specs=pl.BlockSpec((segs, rows, tile), lambda k: (0, 0, k)),
        out_shape=jax.ShapeDtypeStruct((segs, rows, length), jnp.float32),
    )(antenna, members, *table)


def shifted(wide, s, start, rows):
    part = lax.rem(start, 8)
    base = pl.multiple_of(start - part, 8)
    tiles = wide[s, pl.ds(base, rows + 8), :].reshape(rows // 8 + 1, 8, -1)
    turned = pltpu.roll(tiles, lax.rem(8 - part, 8), 1)
    here = lax.broadcasted_iota(jnp.int32, turned[1:].shape, 1) < 8 - part
    return jnp.where(here, turned[:-1], turned[1:]).reshape(rows, -1)


def detect_kernel(last, place_ref, off_ref, near_ref, out_ref, wide):
    segs, rows, length = wide.shape[0], out_ref.shape[1], out_ref.shape[2]
    t = pl.program_id(0)

    @pl.when(t == 0)
    def _():
        wide[:, DMAX : DMAX + rows] = near_ref[:, DMAX : DMAX + rows]
        for s in range(segs):
            low, up = near_ref[s, :DMAX], near_ref[s, DMAX + rows :]
            wide[s, :DMAX] = jnp.where(place_ref[0] == 0, pltpu.roll(low, 1, 1), low)
            wide[s, DMAX + rows : 2 * DMAX + rows] = jnp.where(
                place_ref[0] == last, pltpu.roll(up, length - 1, 1), up
            )

    total = shifted(wide, 0, DMAX + off_ref[t, 0], rows)
    for s in range(1, segs):
        total = total + shifted(wide, s, DMAX + off_ref[t, s], rows)
    out_ref[0] = total / segs


def detect(near, offsets):
    segs, rows, length = near.shape
    rows = rows - 2 * DMAX
    place = lax.axis_index("tm").reshape(1)
    templates = offsets.shape[0]
    smem = pl.BlockSpec(memory_space=pltpu.SMEM)
    return pl.pallas_call(
        functools.partial(detect_kernel, lax.axis_size("tm") - 1),
        grid=(templates,),
        in_specs=[smem, smem, pl.BlockSpec(near.shape, lambda t: (0, 0, 0))],
        out_specs=pl.BlockSpec((1, rows, length), lambda t: (t, 0, 0)),
        out_shape=jax.ShapeDtypeStruct((templates, rows, length), jnp.float32),
        scratch_shapes=[pltpu.VMEM((segs, rows + 3 * DMAX, length), jnp.float32)],
    )(place, offsets, near)


def with_halo(fstat):
    rows = fstat.shape[1]
    count = lax.axis_size("tm")
    up = [(i, (i + 1) % count) for i in range(count)]
    lower = lax.ppermute(fstat[:, rows - DMAX :], "tm", up)
    upper = lax.ppermute(fstat[:, :DMAX], "tm", [(b, a) for a, b in up])
    return jnp.concatenate([lower, fstat, upper], axis=1)


def expand(thin, real_ref, imag_ref):
    high_real, high_imag, low_real, low_imag = thin
    step = low_real.shape[0]

    def body(a, carry):
        real, imag = turned_by(
            high_real[pl.ds(a, 1), :], high_imag[pl.ds(a, 1), :], low_real[...], low_imag[...]
        )
        place = pl.ds(pl.multiple_of(a * step, step), step)
        real_ref[place, :] = real.astype(real_ref.dtype)
        imag_ref[place, :] = imag.astype(imag_ref.dtype)
        return carry

    lax.fori_loop(0, high_real.shape[0], body, 0)


def spectrum_kernel(count, *refs):
    coef, series = refs[:2]
    thin_turn, thin_short, thin_long = refs[2:6], refs[6:10], refs[10:14]
    out = refs[14]
    members, twiddled, arrived, wide = refs[15:19]
    turn_real, turn_imag, short_real, short_imag, long_real, long_imag = refs[19:25]
    go_sem, come_sem, back_sem, land_sem, rim_sem, edge_sem = refs[25:]
    segs, comps, part, length = series.shape
    rows, width = members.shape[2:]
    me = lax.axis_index("tm")
    my_rows = pl.ds(pl.multiple_of(me * part, part), part)
    my_columns = pl.ds(pl.multiple_of(me * width, width), width)
    chunks = [(s, lead) for s in range(segs) for lead in range(0, comps, 2)]

    barrier = pltpu.get_barrier_semaphore()

    def greet(step, carry):
        pl.semaphore_signal(barrier, inc=1, device_id={"tm": lax.rem(me + step, count)})
        return carry

    lax.fori_loop(1, count, greet, 0)
    pl.semaphore_wait(barrier, count - 1)

    for q, (s, lead) in enumerate(chunks):
        pair = pl.ds(lead, 2)

        def send(step, carry):
            peer = lax.rem(me + step, count)
            theirs = pl.ds(pl.multiple_of(peer * width, width), width)
            pltpu.make_async_remote_copy(
                src_ref=series.at[s, pair, :, theirs],
                dst_ref=members.at[s, pair, my_rows, :],
                send_sem=go_sem.at[q],
                recv_sem=come_sem.at[q],
                device_id={"tm": peer},
            ).start()
            return carry

        lax.fori_loop(1, count, send, 0)

    for s in range(segs):
        for c in range(comps):
            members[s, c, my_rows, :] = series[s, c, :, my_columns]
    expand(thin_turn, turn_real, turn_imag)
    expand(thin_short, short_real, short_imag)

    def settle(sem, q):
        some = members.at[0, pl.ds(0, 2), pl.ds(0, (count - 1) * part), :]
        pltpu.make_async_copy(some, some, sem.at[q]).wait()

    expand(thin_long, long_real, long_imag)
    tile = math.gcd(256, rows)
    for q, (s, lead) in enumerate(chunks):
        settle(come_sem, q)
        pair = pl.ds(lead, 2)
        both = jnp.concatenate([members[s, lead], members[s, lead + 1]], axis=-1)

        def strip(r, carry):
            place = pl.ds(pl.multiple_of(r * tile, tile), tile)
            by_real = dot(short_real[place, :], both)
            by_imag = dot(short_imag[place, :], both)
            real, imag = turned_by(
                by_real[:, :width] - by_imag[:, width:],
                by_imag[:, :width] + by_real[:, width:],
                turn_real[place, :],
                turn_imag[place, :],
            )
            twiddled[s, lead, place, :] = real.astype(jnp.bfloat16)
            twiddled[s, lead + 1, place, :] = imag.astype(jnp.bfloat16)
            return carry

        lax.fori_loop(0, rows // tile, strip, 0)

        def send_back(step, carry):
            peer = lax.rem(me + step, count)
            theirs = pl.ds(pl.multiple_of(peer * part, part), part)
            pltpu.make_async_remote_copy(
                src_ref=twiddled.at[s, pair, theirs, :],
                dst_ref=arrived.at[s, pair, :, my_columns],
                send_sem=back_sem.at[q],
                recv_sem=land_sem.at[q],
                device_id={"tm": peer},
            ).start()
            return carry

        lax.fori_loop(1, count, send_back, 0)
        for c in (lead, lead + 1):
            arrived[s, c, :, my_columns] = twiddled[s, c, my_rows, :]

    slab = math.gcd(512, length)
    rims = []
    for s in range(segs):
        for q in range(s * comps // 2, (s + 1) * comps // 2):
            settle(land_sem, q)
        a, b, c = coef[s, 0], coef[s, 1], coef[s, 2]

        def project(k, carry):
            place = pl.ds(pl.multiple_of(k * slab, slab), slab)
            flat = arrived[s].reshape(comps * part, length)
            by_real = dot(flat, long_real[:, place]).reshape(comps, part, slab)
            by_imag = dot(flat, long_imag[:, place]).reshape(comps, part, slab)
            ar, ai = by_real[0] - by_imag[1], by_imag[0] + by_real[1]
            br, bi = by_real[2] - by_imag[3], by_imag[2] + by_real[3]
            numer = (
                b * (ar * ar + ai * ai) + a * (br * br + bi * bi) - 2.0 * c * (ar * br + ai * bi)
            )
            scale = (a * b - c * c) * float(rows * length)
            wide[s, DMAX : DMAX + part, place] = numer / scale
            return carry

        lax.fori_loop(0, length // slab, project, 0)
        for way, (source, target, peer) in enumerate(
            [
                (part, 0, lax.rem(me + 1, count)),
                (DMAX, DMAX + part, lax.rem(me + count - 1, count)),
            ]
        ):
            rim = pltpu.make_async_remote_copy(
                src_ref=wide.at[s, pl.ds(source, DMAX), :],
                dst_ref=wide.at[s, pl.ds(target, DMAX), :],
                send_sem=rim_sem.at[s, way],
                recv_sem=edge_sem.at[s, way],
                device_id={"tm": peer},
            )
            rim.start()
            rims.append(rim)
    for q in range(len(chunks)):
        settle(go_sem, q)
        settle(back_sem, q)
    for rim in rims:
        rim.wait()
    out[...] = wide[...]


def spectrum(series, antenna, count):
    segs, comps, part, length = series.shape
    rows, width = part * count, length // count
    columns = lax.axis_index("tm") * width + jnp.arange(width, dtype=jnp.int32)
    thin = (
        thin_tables(rows * length, columns, rows, 32)
        + thin_tables(rows, jnp.arange(rows, dtype=jnp.int32), rows, 32)
        + thin_tables(length, jnp.arange(length, dtype=jnp.int32), length, 32)
    )
    vmem = pl.BlockSpec(memory_space=pltpu.VMEM)
    half = jnp.bfloat16
    chunks = segs * comps // 2
    dma = pltpu.SemaphoreType.DMA
    near = (segs, part + 2 * DMAX, length)
    return pl.pallas_call(
        functools.partial(spectrum_kernel, count),
        in_specs=[pl.BlockSpec(memory_space=pltpu.SMEM)] + [vmem] * (1 + len(thin)),
        out_specs=vmem,
        out_shape=jax.ShapeDtypeStruct(near, jnp.float32),
        scratch_shapes=[
            pltpu.VMEM((segs, comps, rows, width), half),
            pltpu.VMEM((segs, comps, rows, width), half),
            pltpu.VMEM(series.shape, half),
            pltpu.VMEM(near, jnp.float32),
            pltpu.VMEM((rows, width), jnp.float32),
            pltpu.VMEM((rows, width), jnp.float32),
            pltpu.VMEM((rows, rows), half),
            pltpu.VMEM((rows, rows), half),
            pltpu.VMEM((length, length), half),
            pltpu.VMEM((length, length), half),
            dma((chunks,)),
            dma((chunks,)),
            dma((chunks,)),
            dma((chunks,)),
            dma((segs, 2)),
            dma((segs, 2)),
        ],
        compiler_params=pltpu.CompilerParams(
            collective_id=0, has_side_effects=True, vmem_limit_bytes=60 * 1024 * 1024
        ),
    )(antenna, series, *thin)


def local(series, antenna, offsets):
    count = lax.axis_size("tm")
    rows, length = series.shape[2] * count, series.shape[3]
    width = length // count
    if width % 128 == 0 and series.shape[2] % 32 == 0:
        return detect(spectrum(series, antenna, count), offsets)
    bins = rows * length
    columns = lax.axis_index("tm") * width + jnp.arange(width, dtype=jnp.int32)
    turns = jnp.arange(rows, dtype=jnp.int32)[:, None] * columns[None, :] % bins
    twiddle = unit(turns, bins)
    short, long = dft_table(rows), dft_table(length)
    members = lax.all_to_all(series, "tm", split_axis=3, concat_axis=2, tiled=True)
    twiddled = first_stage(members, short, twiddle)
    members = lax.all_to_all(twiddled, "tm", split_axis=2, concat_axis=3, tiled=True)
    fstat = second_stage(members, long, antenna, bins)
    return detect(with_halo(fstat), offsets)


def solution(mesh):
    return jax.shard_map(
        local,
        mesh=mesh,
        in_specs=(P("sky", None, "tm", None), P("sky", None), P("sky", None)),
        out_specs=P("sky", "tm", None),
        check_vma=False,
    )
```

```python
import functools
import math

import jax
import jax.numpy as jnp
from jax import lax
from jax.experimental import pallas as pl
from jax.experimental.pallas import tpu as pltpu
from jax.sharding import PartitionSpec as P

DMAX = 8
LOW = 64


def unit(products, length):
    angle = products.astype(jnp.float32) * (2.0 * math.pi / length)
    return jnp.cos(angle), -jnp.sin(angle)


def thin_tables(length, columns, rows, low_rows):
    columns = columns[None, :]
    high = low_rows * jnp.arange(rows // low_rows, dtype=jnp.int32)[:, None]
    low = jnp.arange(low_rows, dtype=jnp.int32)[:, None]
    thin = unit(high * columns % length, length) + unit(low * columns % length, length)
    return lax.optimization_barrier(thin)


def turned_by(high_real, high_imag, low_real, low_imag):
    real = high_real * low_real - high_imag * low_imag
    imag = high_real * low_imag + high_imag * low_real
    return real, imag


def dft_table(length):
    thin = thin_tables(length, jnp.arange(length, dtype=jnp.int32), length, LOW)
    real, imag = turned_by(thin[0][:, None], thin[1][:, None], *thin[2:])
    real, imag = real.astype(jnp.bfloat16), imag.astype(jnp.bfloat16)
    return real.reshape(length, length), imag.reshape(length, length)


def dot(x, y):
    return jnp.dot(x, y, preferred_element_type=jnp.float32)


def first_kernel(x_ref, wr_ref, wi_ref, tr_ref, ti_ref, out_ref):
    width = x_ref.shape[-1]
    if width % 128 == 0:
        both = jnp.concatenate([x_ref[0, 0], x_ref[0, 1]], axis=-1)
        by_real = dot(wr_ref[...], both)
        by_imag = dot(wi_ref[...], both)
        real = by_real[:, :width] - by_imag[:, width:]
        imag = by_imag[:, :width] + by_real[:, width:]
    else:
        real = dot(wr_ref[...], x_ref[0, 0]) - dot(wi_ref[...], x_ref[0, 1])
        imag = dot(wi_ref[...], x_ref[0, 0]) + dot(wr_ref[...], x_ref[0, 1])
    tr, ti = tr_ref[...], ti_ref[...]
    out_ref[0, 0] = (real * tr - imag * ti).astype(jnp.bfloat16)
    out_ref[0, 1] = (real * ti + imag * tr).astype(jnp.bfloat16)


def first_stage(members, table, twiddle):
    segs, comps, rows, width = members.shape
    tile = min(256, rows)
    whole = pl.BlockSpec((1, 2, rows, width), lambda s, c, r: (s, c, 0, 0))
    strip = pl.BlockSpec((tile, rows), lambda s, c, r: (r, 0))
    turn = pl.BlockSpec((tile, width), lambda s, c, r: (r, 0))
    return pl.pallas_call(
        first_kernel,
        grid=(segs, comps // 2, rows // tile),
        in_specs=[whole, strip, strip, turn, turn],
        out_specs=pl.BlockSpec((1, 2, tile, width), lambda s, c, r: (s, c, r, 0)),
        out_shape=jax.ShapeDtypeStruct(members.shape, jnp.bfloat16),
    )(members, *table, *twiddle)


def second_kernel(bins, coef_ref, x_ref, wr_ref, wi_ref, out_ref):
    segs, comps, rows, length = x_ref.shape
    flat = x_ref[...].reshape(segs * comps * rows, length)
    by_real = dot(flat, wr_ref[...]).reshape(segs, comps, rows, -1)
    by_imag = dot(flat, wi_ref[...]).reshape(segs, comps, rows, -1)
    for s in range(segs):
        ar = by_real[s, 0] - by_imag[s, 1]
        ai = by_imag[s, 0] + by_real[s, 1]
        br = by_real[s, 2] - by_imag[s, 3]
        bi = by_imag[s, 2] + by_real[s, 3]
        a, b, c = coef_ref[s, 0], coef_ref[s, 1], coef_ref[s, 2]
        numer = b * (ar * ar + ai * ai) + a * (br * br + bi * bi) - 2.0 * c * (ar * br + ai * bi)
        out_ref[s] = numer / ((a * b - c * c) * bins)


def second_stage(members, table, antenna, bins):
    segs, comps, rows, length = members.shape
    tile = min(512, length)
    column = pl.BlockSpec((length, tile), lambda k: (0, k))
    return pl.pallas_call(
        functools.partial(second_kernel, float(bins)),
        grid=(length // tile,),
        in_specs=[
            pl.BlockSpec(memory_space=pltpu.SMEM),
            pl.BlockSpec(members.shape, lambda k: (0, 0, 0, 0)),
            column,
            column,
        ],
        out_specs=pl.BlockSpec((segs, rows, tile), lambda k: (0, 0, k)),
        out_shape=jax.ShapeDtypeStruct((segs, rows, length), jnp.float32),
    )(antenna, members, *table)


def shifted(wide, s, start, rows):
    part = lax.rem(start, 8)
    base = pl.multiple_of(start - part, 8)
    tiles = wide[s, pl.ds(base, rows + 8), :].reshape(rows // 8 + 1, 8, -1)
    turned = pltpu.roll(tiles, lax.rem(8 - part, 8), 1)
    here = lax.broadcasted_iota(jnp.int32, turned[1:].shape, 1) < 8 - part
    return jnp.where(here, turned[:-1], turned[1:]).reshape(rows, -1)


def detect_kernel(last, place_ref, off_ref, near_ref, out_ref, wide):
    segs, rows, length = wide.shape[0], out_ref.shape[1], out_ref.shape[2]
    t = pl.program_id(0)

    @pl.when(t == 0)
    def _():
        wide[:, DMAX : DMAX + rows] = near_ref[:, DMAX : DMAX + rows]
        for s in range(segs):
            low, up = near_ref[s, :DMAX], near_ref[s, DMAX + rows :]
            wide[s, :DMAX] = jnp.where(place_ref[0] == 0, pltpu.roll(low, 1, 1), low)
            wide[s, DMAX + rows : 2 * DMAX + rows] = jnp.where(
                place_ref[0] == last, pltpu.roll(up, length - 1, 1), up
            )

    total = shifted(wide, 0, DMAX + off_ref[0, t], rows)
    for s in range(1, segs):
        total = total + shifted(wide, s, DMAX + off_ref[s, t], rows)
    out_ref[0] = total / segs


def detect(near, offsets):
    segs, rows, length = near.shape
    rows = rows - 2 * DMAX
    place = lax.axis_index("tm").reshape(1)
    templates = offsets.shape[0]
    smem = pl.BlockSpec(memory_space=pltpu.SMEM)
    return pl.pallas_call(
        functools.partial(detect_kernel, lax.axis_size("tm") - 1),
        grid=(templates,),
        in_specs=[smem, smem, pl.BlockSpec(near.shape, lambda t: (0, 0, 0))],
        out_specs=pl.BlockSpec((1, rows, length), lambda t: (t, 0, 0)),
        out_shape=jax.ShapeDtypeStruct((templates, rows, length), jnp.float32),
        scratch_shapes=[pltpu.VMEM((segs, rows + 3 * DMAX, length), jnp.float32)],
    )(place, offsets.T, near)


def with_halo(fstat):
    rows = fstat.shape[1]
    count = lax.axis_size("tm")
    up = [(i, (i + 1) % count) for i in range(count)]
    lower = lax.ppermute(fstat[:, rows - DMAX :], "tm", up)
    upper = lax.ppermute(fstat[:, :DMAX], "tm", [(b, a) for a, b in up])
    return jnp.concatenate([lower, fstat, upper], axis=1)


def expand(length, first, thin, real_ref, imag_ref):
    high_real, high_imag, low_real, low_imag = thin
    step = low_real.shape[0]
    for scale, real, imag in ((step, high_real, high_imag), (1, low_real, low_imag)):
        rows = scale * lax.broadcasted_iota(jnp.int32, real.shape, 0)
        columns = first + lax.broadcasted_iota(jnp.int32, real.shape, 1)
        real[...], imag[...] = unit(lax.rem(rows * columns, jnp.full_like(rows, length)), length)

    def body(a, carry):
        real, imag = turned_by(
            high_real[pl.ds(a, 1), :], high_imag[pl.ds(a, 1), :], low_real[...], low_imag[...]
        )
        place = pl.ds(pl.multiple_of(a * step, step), step)
        real_ref[place, :] = real.astype(real_ref.dtype)
        imag_ref[place, :] = imag.astype(imag_ref.dtype)
        return carry

    lax.fori_loop(0, high_real.shape[0], body, 0)


def spectrum_kernel(count, *refs):
    coef, series, out = refs[:3]
    members, twiddled, arrived, wide = refs[3:7]
    turn_real, turn_imag, short_real, short_imag, long_real, long_imag = refs[7:13]
    go_sem, come_sem, back_sem, land_sem, rim_sem, edge_sem = refs[13:19]
    thin_turn, thin_short, thin_long = refs[19:23], refs[23:27], refs[27:31]
    segs, comps, part, length = series.shape
    rows, width = members.shape[2:]
    me = lax.axis_index("tm")
    my_rows = pl.ds(pl.multiple_of(me * part, part), part)
    my_columns = pl.ds(pl.multiple_of(me * width, width), width)
    chunks = [(s, lead) for s in range(segs) for lead in range(0, comps, 2)]

    barrier = pltpu.get_barrier_semaphore()

    def greet(step, carry):
        pl.semaphore_signal(barrier, inc=1, device_id={"tm": lax.rem(me + step, count)})
        return carry

    def to_each(start):
        if count % 2:
            return lax.fori_loop(1, count, lambda n, c: start(lax.rem(me + n, count), c), 0)
        mid = count // 2
        side, seat = me // mid, lax.rem(me, mid)

        def body(n, carry):
            turn = lax.rem(seat + n, mid)
            start(side * mid + turn, carry)
            return start((1 - side) * mid + turn, carry)

        start((1 - side) * mid + seat, 0)
        return lax.fori_loop(1, mid, body, 0)

    lax.fori_loop(1, count, greet, 0)
    pl.semaphore_wait(barrier, count - 1)

    for q, (s, lead) in enumerate(chunks):
        pair = pl.ds(lead, 2)

        def send(peer, carry):
            theirs = pl.ds(pl.multiple_of(peer * width, width), width)
            pltpu.make_async_remote_copy(
                src_ref=series.at[s, pair, :, theirs],
                dst_ref=members.at[s, pair, my_rows, :],
                send_sem=go_sem.at[q],
                recv_sem=come_sem.at[q],
                device_id={"tm": peer},
            ).start()
            return carry

        to_each(send)

    for s in range(segs):
        for c in range(comps):
            members[s, c, my_rows, :] = series[s, c, :, my_columns]
    expand(rows * length, me * width, thin_turn, turn_real, turn_imag)
    expand(rows, 0, thin_short, short_real, short_imag)

    def settle(sem, q):
        some = members.at[0, pl.ds(0, 2), pl.ds(0, (count - 1) * part), :]
        pltpu.make_async_copy(some, some, sem.at[q]).wait()

    tile = math.gcd(256, rows)
    for q, (s, lead) in enumerate(chunks):
        settle(come_sem, q)
        pair = pl.ds(lead, 2)
        both = jnp.concatenate([members[s, lead], members[s, lead + 1]], axis=-1)

        def strip(r, carry):
            place = pl.ds(pl.multiple_of(r * tile, tile), tile)
            by_real = dot(short_real[place, :], both)
            by_imag = dot(short_imag[place, :], both)
            real, imag = turned_by(
                by_real[:, :width] - by_imag[:, width:],
                by_imag[:, :width] + by_real[:, width:],
                turn_real[place, :],
                turn_imag[place, :],
            )
            twiddled[s, lead, place, :] = real.astype(jnp.bfloat16)
            twiddled[s, lead + 1, place, :] = imag.astype(jnp.bfloat16)
            return carry

        lax.fori_loop(0, rows // tile, strip, 0)

        def send_back(peer, carry):
            theirs = pl.ds(pl.multiple_of(peer * part, part), part)
            pltpu.make_async_remote_copy(
                src_ref=twiddled.at[s, pair, theirs, :],
                dst_ref=arrived.at[s, pair, :, my_columns],
                send_sem=back_sem.at[q],
                recv_sem=land_sem.at[q],
                device_id={"tm": peer},
            ).start()
            return carry

        to_each(send_back)
        for c in (lead, lead + 1):
            arrived[s, c, :, my_columns] = twiddled[s, c, my_rows, :]
        if q == 0:
            expand(length, 0, thin_long, long_real, long_imag)

    slab = math.gcd(512, length)
    rims = []
    for s in range(segs):
        for q in range(s * comps // 2, (s + 1) * comps // 2):
            settle(land_sem, q)
        a, b, c = coef[s, 0], coef[s, 1], coef[s, 2]

        def project(k, carry):
            place = pl.ds(pl.multiple_of(k * slab, slab), slab)
            flat = arrived[s].reshape(comps * part, length)
            by_real = dot(flat, long_real[:, place]).reshape(comps, part, slab)
            by_imag = dot(flat, long_imag[:, place]).reshape(comps, part, slab)
            ar, ai = by_real[0] - by_imag[1], by_imag[0] + by_real[1]
            br, bi = by_real[2] - by_imag[3], by_imag[2] + by_real[3]
            numer = (
                b * (ar * ar + ai * ai) + a * (br * br + bi * bi) - 2.0 * c * (ar * br + ai * bi)
            )
            scale = (a * b - c * c) * float(rows * length)
            wide[s, DMAX : DMAX + part, place] = numer / scale
            return carry

        lax.fori_loop(0, length // slab, project, 0)
        for way, (source, target, peer) in enumerate(
            [
                (part, 0, lax.rem(me + 1, count)),
                (DMAX, DMAX + part, lax.rem(me + count - 1, count)),
            ]
        ):
            rim = pltpu.make_async_remote_copy(
                src_ref=wide.at[s, pl.ds(source, DMAX), :],
                dst_ref=wide.at[s, pl.ds(target, DMAX), :],
                send_sem=rim_sem.at[s, way],
                recv_sem=edge_sem.at[s, way],
                device_id={"tm": peer},
            )
            rim.start()
            rims.append(rim)
    for q in range(len(chunks)):
        settle(go_sem, q)
        settle(back_sem, q)
    for rim in rims:
        rim.wait()
    out[...] = wide[...]


def spectrum(series, antenna, count):
    segs, comps, part, length = series.shape
    rows, width = part * count, length // count
    vmem = pl.BlockSpec(memory_space=pltpu.VMEM)
    half = jnp.bfloat16

    def thin(tall, across):
        return [pltpu.VMEM((n, across), jnp.float32) for n in (tall // 32, tall // 32, 32, 32)]

    chunks = segs * comps // 2
    dma = pltpu.SemaphoreType.DMA
    near = (segs, part + 2 * DMAX, length)
    return pl.pallas_call(
        functools.partial(spectrum_kernel, count),
        in_specs=[pl.BlockSpec(memory_space=pltpu.SMEM)] + [vmem],
        out_specs=vmem,
        out_shape=jax.ShapeDtypeStruct(near, jnp.float32),
        scratch_shapes=[
            pltpu.VMEM((segs, comps, rows, width), half),
            pltpu.VMEM((segs, comps, rows, width), half),
            pltpu.VMEM(series.shape, half),
            pltpu.VMEM(near, jnp.float32),
            pltpu.VMEM((rows, width), jnp.float32),
            pltpu.VMEM((rows, width), jnp.float32),
            pltpu.VMEM((rows, rows), half),
            pltpu.VMEM((rows, rows), half),
            pltpu.VMEM((length, length), half),
            pltpu.VMEM((length, length), half),
            dma((chunks,)),
            dma((chunks,)),
            dma((chunks,)),
            dma((chunks,)),
            dma((segs, 2)),
            dma((segs, 2)),
        ]
        + thin(rows, width)
        + thin(rows, rows)
        + thin(length, length),
        compiler_params=pltpu.CompilerParams(
            collective_id=0, has_side_effects=True, vmem_limit_bytes=60 * 1024 * 1024
        ),
    )(antenna, series)


def local(series, antenna, offsets):
    count = lax.axis_size("tm")
    rows, length = series.shape[2] * count, series.shape[3]
    width = length // count
    if width % 128 == 0 and series.shape[2] % 32 == 0:
        return detect(spectrum(series, antenna, count), offsets)
    bins = rows * length
    columns = lax.axis_index("tm") * width + jnp.arange(width, dtype=jnp.int32)
    turns = jnp.arange(rows, dtype=jnp.int32)[:, None] * columns[None, :] % bins
    twiddle = unit(turns, bins)
    short, long = dft_table(rows), dft_table(length)
    members = lax.all_to_all(series, "tm", split_axis=3, concat_axis=2, tiled=True)
    twiddled = first_stage(members, short, twiddle)
    members = lax.all_to_all(twiddled, "tm", split_axis=2, concat_axis=3, tiled=True)
    fstat = second_stage(members, long, antenna, bins)
    return detect(with_halo(fstat), offsets)


def solution(mesh):
    return jax.shard_map(
        local,
        mesh=mesh,
        in_specs=(P("sky", None, "tm", None), P("sky", None), P("sky", None)),
        out_specs=P("sky", "tm", None),
        check_vma=False,
    )
```

```python
import functools
import math

import jax
import jax.numpy as jnp
from jax import lax
from jax.experimental import pallas as pl
from jax.experimental.pallas import tpu as pltpu
from jax.sharding import PartitionSpec as P

DMAX = 8
LOW = 64


def unit(products, length):
    angle = products.astype(jnp.float32) * (2.0 * math.pi / length)
    return jnp.cos(angle), -jnp.sin(angle)


def thin_tables(length, columns, rows, low_rows):
    columns = columns[None, :]
    high = low_rows * jnp.arange(rows // low_rows, dtype=jnp.int32)[:, None]
    low = jnp.arange(low_rows, dtype=jnp.int32)[:, None]
    thin = unit(high * columns % length, length) + unit(low * columns % length, length)
    return lax.optimization_barrier(thin)


def turned_by(high_real, high_imag, low_real, low_imag):
    real = high_real * low_real - high_imag * low_imag
    imag = high_real * low_imag + high_imag * low_real
    return real, imag


def dft_table(length):
    thin = thin_tables(length, jnp.arange(length, dtype=jnp.int32), length, LOW)
    real, imag = turned_by(thin[0][:, None], thin[1][:, None], *thin[2:])
    real, imag = real.astype(jnp.bfloat16), imag.astype(jnp.bfloat16)
    return real.reshape(length, length), imag.reshape(length, length)


def dot(x, y):
    return jnp.dot(x, y, preferred_element_type=jnp.float32)


def first_kernel(x_ref, wr_ref, wi_ref, tr_ref, ti_ref, out_ref):
    width = x_ref.shape[-1]
    if width % 128 == 0:
        both = jnp.concatenate([x_ref[0, 0], x_ref[0, 1]], axis=-1)
        by_real = dot(wr_ref[...], both)
        by_imag = dot(wi_ref[...], both)
        real = by_real[:, :width] - by_imag[:, width:]
        imag = by_imag[:, :width] + by_real[:, width:]
    else:
        real = dot(wr_ref[...], x_ref[0, 0]) - dot(wi_ref[...], x_ref[0, 1])
        imag = dot(wi_ref[...], x_ref[0, 0]) + dot(wr_ref[...], x_ref[0, 1])
    tr, ti = tr_ref[...], ti_ref[...]
    out_ref[0, 0] = (real * tr - imag * ti).astype(jnp.bfloat16)
    out_ref[0, 1] = (real * ti + imag * tr).astype(jnp.bfloat16)


def first_stage(members, table, twiddle):
    segs, comps, rows, width = members.shape
    tile = min(256, rows)
    whole = pl.BlockSpec((1, 2, rows, width), lambda s, c, r: (s, c, 0, 0))
    strip = pl.BlockSpec((tile, rows), lambda s, c, r: (r, 0))
    turn = pl.BlockSpec((tile, width), lambda s, c, r: (r, 0))
    return pl.pallas_call(
        first_kernel,
        grid=(segs, comps // 2, rows // tile),
        in_specs=[whole, strip, strip, turn, turn],
        out_specs=pl.BlockSpec((1, 2, tile, width), lambda s, c, r: (s, c, r, 0)),
        out_shape=jax.ShapeDtypeStruct(members.shape, jnp.bfloat16),
    )(members, *table, *twiddle)


def second_kernel(bins, coef_ref, x_ref, wr_ref, wi_ref, out_ref):
    segs, comps, rows, length = x_ref.shape
    flat = x_ref[...].reshape(segs * comps * rows, length)
    by_real = dot(flat, wr_ref[...]).reshape(segs, comps, rows, -1)
    by_imag = dot(flat, wi_ref[...]).reshape(segs, comps, rows, -1)
    for s in range(segs):
        ar = by_real[s, 0] - by_imag[s, 1]
        ai = by_imag[s, 0] + by_real[s, 1]
        br = by_real[s, 2] - by_imag[s, 3]
        bi = by_imag[s, 2] + by_real[s, 3]
        a, b, c = coef_ref[s, 0], coef_ref[s, 1], coef_ref[s, 2]
        numer = b * (ar * ar + ai * ai) + a * (br * br + bi * bi) - 2.0 * c * (ar * br + ai * bi)
        out_ref[s] = numer / ((a * b - c * c) * bins)


def second_stage(members, table, antenna, bins):
    segs, comps, rows, length = members.shape
    tile = min(512, length)
    column = pl.BlockSpec((length, tile), lambda k: (0, k))
    return pl.pallas_call(
        functools.partial(second_kernel, float(bins)),
        grid=(length // tile,),
        in_specs=[
            pl.BlockSpec(memory_space=pltpu.SMEM),
            pl.BlockSpec(members.shape, lambda k: (0, 0, 0, 0)),
            column,
            column,
        ],
        out_specs=pl.BlockSpec((segs, rows, tile), lambda k: (0, 0, k)),
        out_shape=jax.ShapeDtypeStruct((segs, rows, length), jnp.float32),
    )(antenna, members, *table)


def shifted(wide, s, start, rows):
    part = lax.rem(start, 8)
    base = pl.multiple_of(start - part, 8)
    tiles = wide[s, pl.ds(base, rows + 8), :].reshape(rows // 8 + 1, 8, -1)
    turned = pltpu.roll(tiles, lax.rem(8 - part, 8), 1)
    here = lax.broadcasted_iota(jnp.int32, turned[1:].shape, 1) < 8 - part
    return jnp.where(here, turned[:-1], turned[1:]).reshape(rows, -1)


def detect_kernel(last, place_ref, off_ref, near_ref, out_ref, wide):
    segs, rows, length = wide.shape[0], out_ref.shape[1], out_ref.shape[2]
    t = pl.program_id(0)

    @pl.when(t == 0)
    def _():
        wide[:, DMAX : DMAX + rows] = near_ref[:, DMAX : DMAX + rows]
        for s in range(segs):
            low, up = near_ref[s, :DMAX], near_ref[s, DMAX + rows :]
            wide[s, :DMAX] = jnp.where(place_ref[0] == 0, pltpu.roll(low, 1, 1), low)
            wide[s, DMAX + rows : 2 * DMAX + rows] = jnp.where(
                place_ref[0] == last, pltpu.roll(up, length - 1, 1), up
            )

    total = shifted(wide, 0, DMAX + off_ref[0, t], rows)
    for s in range(1, segs):
        total = total + shifted(wide, s, DMAX + off_ref[s, t], rows)
    out_ref[0] = total / segs


def detect(near, offsets):
    segs, rows, length = near.shape
    rows = rows - 2 * DMAX
    place = lax.axis_index("tm").reshape(1)
    templates = offsets.shape[0]
    smem = pl.BlockSpec(memory_space=pltpu.SMEM)
    return pl.pallas_call(
        functools.partial(detect_kernel, lax.axis_size("tm") - 1),
        grid=(templates,),
        in_specs=[smem, smem, pl.BlockSpec(near.shape, lambda t: (0, 0, 0))],
        out_specs=pl.BlockSpec((1, rows, length), lambda t: (t, 0, 0)),
        out_shape=jax.ShapeDtypeStruct((templates, rows, length), jnp.float32),
        scratch_shapes=[pltpu.VMEM((segs, rows + 3 * DMAX, length), jnp.float32)],
    )(place, offsets.T, near)


def with_halo(fstat):
    rows = fstat.shape[1]
    count = lax.axis_size("tm")
    up = [(i, (i + 1) % count) for i in range(count)]
    lower = lax.ppermute(fstat[:, rows - DMAX :], "tm", up)
    upper = lax.ppermute(fstat[:, :DMAX], "tm", [(b, a) for a, b in up])
    return jnp.concatenate([lower, fstat, upper], axis=1)


def expand(length, first, thin, real_ref, imag_ref):
    high_real, high_imag, low_real, low_imag = thin
    step = low_real.shape[0]
    for scale, real, imag in ((step, high_real, high_imag), (1, low_real, low_imag)):
        rows = scale * lax.broadcasted_iota(jnp.int32, real.shape, 0)
        columns = first + lax.broadcasted_iota(jnp.int32, real.shape, 1)
        real[...], imag[...] = unit(lax.rem(rows * columns, jnp.full_like(rows, length)), length)

    def body(a, carry):
        real, imag = turned_by(
            high_real[pl.ds(a, 1), :], high_imag[pl.ds(a, 1), :], low_real[...], low_imag[...]
        )
        place = pl.ds(pl.multiple_of(a * step, step), step)
        real_ref[place, :] = real.astype(real_ref.dtype)
        imag_ref[place, :] = imag.astype(imag_ref.dtype)
        return carry

    lax.fori_loop(0, high_real.shape[0], body, 0)


def spectrum_kernel(count, *refs):
    coef, given, out = refs[:3]
    members, twiddled, arrived, wide = refs[3:7]
    turn_real, turn_imag, short_real, short_imag, long_real, long_imag = refs[7:13]
    go_sem, come_sem, back_sem, land_sem, rim_sem, edge_sem = refs[13:19]
    thin_turn, thin_short, thin_long = refs[19:23], refs[23:27], refs[27:31]
    series, field, load_sem = refs[31:]
    segs, comps, part, length = series.shape
    rows, width = members.shape[2:]
    me = lax.axis_index("tm")
    my_rows = pl.ds(pl.multiple_of(me * part, part), part)
    my_columns = pl.ds(pl.multiple_of(me * width, width), width)
    chunks = [(s, lead) for s in range(segs) for lead in range(0, comps, 2)]

    load = pltpu.make_async_copy(given, series, load_sem)
    load.start()
    barrier = pltpu.get_barrier_semaphore()

    def greet(step, carry):
        pl.semaphore_signal(barrier, inc=1, device_id={"tm": lax.rem(me + step, count)})
        return carry

    def to_each(start):
        if count % 2:
            return lax.fori_loop(1, count, lambda n, c: start(lax.rem(me + n, count), c), 0)
        mid = count // 2
        side, seat = me // mid, lax.rem(me, mid)

        def body(n, carry):
            turn = lax.rem(seat + n, mid)
            start(side * mid + turn, carry)
            return start((1 - side) * mid + turn, carry)

        start((1 - side) * mid + seat, 0)
        return lax.fori_loop(1, mid, body, 0)

    lax.fori_loop(1, count, greet, 0)
    pl.semaphore_wait(barrier, count - 1)
    load.wait()

    for q, (s, lead) in enumerate(chunks):
        pair = pl.ds(lead, 2)

        def send(peer, carry):
            theirs = pl.ds(pl.multiple_of(peer * width, width), width)
            pltpu.make_async_remote_copy(
                src_ref=series.at[s, pair, :, theirs],
                dst_ref=members.at[s, pair, my_rows, :],
                send_sem=go_sem.at[q],
                recv_sem=come_sem.at[q],
                device_id={"tm": peer},
            ).start()
            return carry

        to_each(send)

    for s in range(segs):
        for c in range(comps):
            members[s, c, my_rows, :] = series[s, c, :, my_columns]
    expand(rows * length, me * width, thin_turn, turn_real, turn_imag)
    expand(rows, 0, thin_short, short_real, short_imag)

    def settle(sem, q):
        some = members.at[0, pl.ds(0, 2), pl.ds(0, (count - 1) * part), :]
        pltpu.make_async_copy(some, some, sem.at[q]).wait()

    tile = math.gcd(256, rows)
    for q, (s, lead) in enumerate(chunks):
        settle(come_sem, q)
        pair = pl.ds(lead, 2)
        both = jnp.concatenate([members[s, lead], members[s, lead + 1]], axis=-1)

        def strip(r, carry):
            place = pl.ds(pl.multiple_of(r * tile, tile), tile)
            by_real = dot(short_real[place, :], both)
            by_imag = dot(short_imag[place, :], both)
            real, imag = turned_by(
                by_real[:, :width] - by_imag[:, width:],
                by_imag[:, :width] + by_real[:, width:],
                turn_real[place, :],
                turn_imag[place, :],
            )
            twiddled[s, lead, place, :] = real.astype(jnp.bfloat16)
            twiddled[s, lead + 1, place, :] = imag.astype(jnp.bfloat16)
            return carry

        lax.fori_loop(0, rows // tile, strip, 0)

        def send_back(peer, carry):
            theirs = pl.ds(pl.multiple_of(peer * part, part), part)
            pltpu.make_async_remote_copy(
                src_ref=twiddled.at[s, pair, theirs, :],
                dst_ref=arrived.at[s, pair, :, my_columns],
                send_sem=back_sem.at[q],
                recv_sem=land_sem.at[q],
                device_id={"tm": peer},
            ).start()
            return carry

        to_each(send_back)
        for c in (lead, lead + 1):
            arrived[s, c, :, my_columns] = twiddled[s, c, my_rows, :]
        if q == 0:
            expand(length, 0, thin_long, long_real, long_imag)

    slab = math.gcd(512, length)
    rims = []
    last = comps - 2
    for q, (s, lead) in enumerate(chunks):
        settle(land_sem, q)
        a, b, c = coef[s, 0], coef[s, 1], coef[s, 2]

        def project(k, carry):
            place = pl.ds(pl.multiple_of(k * slab, slab), slab)
            flat = arrived[s, lead : lead + 2].reshape(2 * part, length)
            by_real = dot(flat, long_real[:, place])
            by_imag = dot(flat, long_imag[:, place])
            real, imag = by_real[:part] - by_imag[part:], by_imag[:part] + by_real[part:]
            if lead != last:
                field[0, :, place] = real
                field[1, :, place] = imag
                return carry
            ar, ai, br, bi = field[0, :, place], field[1, :, place], real, imag
            numer = (
                b * (ar * ar + ai * ai) + a * (br * br + bi * bi) - 2.0 * c * (ar * br + ai * bi)
            )
            scale = (a * b - c * c) * float(rows * length)
            wide[s, DMAX : DMAX + part, place] = numer / scale
            return carry

        lax.fori_loop(0, length // slab, project, 0)
        if lead != last:
            continue
        for way, (source, target, peer) in enumerate(
            [
                (part, 0, lax.rem(me + 1, count)),
                (DMAX, DMAX + part, lax.rem(me + count - 1, count)),
            ]
        ):
            rim = pltpu.make_async_remote_copy(
                src_ref=wide.at[s, pl.ds(source, DMAX), :],
                dst_ref=wide.at[s, pl.ds(target, DMAX), :],
                send_sem=rim_sem.at[s, way],
                recv_sem=edge_sem.at[s, way],
                device_id={"tm": peer},
            )
            rim.start()
            rims.append(rim)
    for q in range(len(chunks)):
        settle(go_sem, q)
        settle(back_sem, q)
    own = slice(DMAX, DMAX + part)
    out[:, own] = wide[:, own]
    for rim in rims:
        rim.wait()
    out[:, :DMAX] = wide[:, :DMAX]
    out[:, DMAX + part :] = wide[:, DMAX + part :]


def spectrum(series, antenna, count):
    segs, comps, part, length = series.shape
    rows, width = part * count, length // count
    vmem = pl.BlockSpec(memory_space=pltpu.VMEM)
    half = jnp.bfloat16

    def thin(tall, across):
        return [pltpu.VMEM((n, across), jnp.float32) for n in (tall // 32, tall // 32, 32, 32)]

    chunks = segs * comps // 2
    dma = pltpu.SemaphoreType.DMA
    near = (segs, part + 2 * DMAX, length)
    return pl.pallas_call(
        functools.partial(spectrum_kernel, count),
        in_specs=[pl.BlockSpec(memory_space=pltpu.SMEM), pl.BlockSpec(memory_space=pl.ANY)],
        out_specs=vmem,
        out_shape=jax.ShapeDtypeStruct(near, jnp.float32),
        scratch_shapes=[
            pltpu.VMEM((segs, comps, rows, width), half),
            pltpu.VMEM((segs, comps, rows, width), half),
            pltpu.VMEM(series.shape, half),
            pltpu.VMEM(near, jnp.float32),
            pltpu.VMEM((rows, width), jnp.float32),
            pltpu.VMEM((rows, width), jnp.float32),
            pltpu.VMEM((rows, rows), half),
            pltpu.VMEM((rows, rows), half),
            pltpu.VMEM((length, length), half),
            pltpu.VMEM((length, length), half),
            dma((chunks,)),
            dma((chunks,)),
            dma((chunks,)),
            dma((chunks,)),
            dma((segs, 2)),
            dma((segs, 2)),
        ]
        + thin(rows, width)
        + thin(rows, rows)
        + thin(length, length)
        + [
            pltpu.VMEM(series.shape, half),
            pltpu.VMEM((2, part, length), jnp.float32),
            dma,
        ],
        compiler_params=pltpu.CompilerParams(
            collective_id=0, has_side_effects=True, vmem_limit_bytes=60 * 1024 * 1024
        ),
    )(antenna, series)


def local(series, antenna, offsets):
    count = lax.axis_size("tm")
    rows, length = series.shape[2] * count, series.shape[3]
    width = length // count
    if width % 128 == 0 and series.shape[2] % 32 == 0:
        return detect(spectrum(series, antenna, count), offsets)
    bins = rows * length
    columns = lax.axis_index("tm") * width + jnp.arange(width, dtype=jnp.int32)
    turns = jnp.arange(rows, dtype=jnp.int32)[:, None] * columns[None, :] % bins
    twiddle = unit(turns, bins)
    short, long = dft_table(rows), dft_table(length)
    members = lax.all_to_all(series, "tm", split_axis=3, concat_axis=2, tiled=True)
    twiddled = first_stage(members, short, twiddle)
    members = lax.all_to_all(twiddled, "tm", split_axis=2, concat_axis=3, tiled=True)
    fstat = second_stage(members, long, antenna, bins)
    return detect(with_halo(fstat), offsets)


def solution(mesh):
    return jax.shard_map(
        local,
        mesh=mesh,
        in_specs=(P("sky", None, "tm", None), P("sky", None), P("sky", None)),
        out_specs=P("sky", "tm", None),
        check_vma=False,
    )
```

```python
import functools
import math

import jax
import jax.numpy as jnp
from jax import lax
from jax.experimental import pallas as pl
from jax.experimental.pallas import tpu as pltpu
from jax.sharding import PartitionSpec as P

DMAX = 8
LOW = 64


def unit(products, length):
    angle = products.astype(jnp.float32) * (2.0 * math.pi / length)
    return jnp.cos(angle), -jnp.sin(angle)


def thin_tables(length, columns, rows, low_rows):
    columns = columns[None, :]
    high = low_rows * jnp.arange(rows // low_rows, dtype=jnp.int32)[:, None]
    low = jnp.arange(low_rows, dtype=jnp.int32)[:, None]
    thin = unit(high * columns % length, length) + unit(low * columns % length, length)
    return lax.optimization_barrier(thin)


def turned_by(high_real, high_imag, low_real, low_imag):
    real = high_real * low_real - high_imag * low_imag
    imag = high_real * low_imag + high_imag * low_real
    return real, imag


def dft_table(length):
    thin = thin_tables(length, jnp.arange(length, dtype=jnp.int32), length, LOW)
    real, imag = turned_by(thin[0][:, None], thin[1][:, None], *thin[2:])
    real, imag = real.astype(jnp.bfloat16), imag.astype(jnp.bfloat16)
    return real.reshape(length, length), imag.reshape(length, length)


def dot(x, y):
    return jnp.dot(x, y, preferred_element_type=jnp.float32)


def first_kernel(x_ref, wr_ref, wi_ref, tr_ref, ti_ref, out_ref):
    width = x_ref.shape[-1]
    if width % 128 == 0:
        both = jnp.concatenate([x_ref[0, 0], x_ref[0, 1]], axis=-1)
        by_real = dot(wr_ref[...], both)
        by_imag = dot(wi_ref[...], both)
        real = by_real[:, :width] - by_imag[:, width:]
        imag = by_imag[:, :width] + by_real[:, width:]
    else:
        real = dot(wr_ref[...], x_ref[0, 0]) - dot(wi_ref[...], x_ref[0, 1])
        imag = dot(wi_ref[...], x_ref[0, 0]) + dot(wr_ref[...], x_ref[0, 1])
    tr, ti = tr_ref[...], ti_ref[...]
    out_ref[0, 0] = (real * tr - imag * ti).astype(jnp.bfloat16)
    out_ref[0, 1] = (real * ti + imag * tr).astype(jnp.bfloat16)


def first_stage(members, table, twiddle):
    segs, comps, rows, width = members.shape
    tile = min(256, rows)
    whole = pl.BlockSpec((1, 2, rows, width), lambda s, c, r: (s, c, 0, 0))
    strip = pl.BlockSpec((tile, rows), lambda s, c, r: (r, 0))
    turn = pl.BlockSpec((tile, width), lambda s, c, r: (r, 0))
    return pl.pallas_call(
        first_kernel,
        grid=(segs, comps // 2, rows // tile),
        in_specs=[whole, strip, strip, turn, turn],
        out_specs=pl.BlockSpec((1, 2, tile, width), lambda s, c, r: (s, c, r, 0)),
        out_shape=jax.ShapeDtypeStruct(members.shape, jnp.bfloat16),
    )(members, *table, *twiddle)


def second_kernel(bins, coef_ref, x_ref, wr_ref, wi_ref, out_ref):
    segs, comps, rows, length = x_ref.shape
    flat = x_ref[...].reshape(segs * comps * rows, length)
    by_real = dot(flat, wr_ref[...]).reshape(segs, comps, rows, -1)
    by_imag = dot(flat, wi_ref[...]).reshape(segs, comps, rows, -1)
    for s in range(segs):
        ar = by_real[s, 0] - by_imag[s, 1]
        ai = by_imag[s, 0] + by_real[s, 1]
        br = by_real[s, 2] - by_imag[s, 3]
        bi = by_imag[s, 2] + by_real[s, 3]
        a, b, c = coef_ref[s, 0], coef_ref[s, 1], coef_ref[s, 2]
        numer = b * (ar * ar + ai * ai) + a * (br * br + bi * bi) - 2.0 * c * (ar * br + ai * bi)
        out_ref[s] = numer / ((a * b - c * c) * bins)


def second_stage(members, table, antenna, bins):
    segs, comps, rows, length = members.shape
    tile = min(512, length)
    column = pl.BlockSpec((length, tile), lambda k: (0, k))
    return pl.pallas_call(
        functools.partial(second_kernel, float(bins)),
        grid=(length // tile,),
        in_specs=[
            pl.BlockSpec(memory_space=pltpu.SMEM),
            pl.BlockSpec(members.shape, lambda k: (0, 0, 0, 0)),
            column,
            column,
        ],
        out_specs=pl.BlockSpec((segs, rows, tile), lambda k: (0, 0, k)),
        out_shape=jax.ShapeDtypeStruct((segs, rows, length), jnp.float32),
    )(antenna, members, *table)


def shifted(wide, s, start, rows):
    part = lax.rem(start, 8)
    base = pl.multiple_of(start - part, 8)
    tiles = wide[s, pl.ds(base, rows + 8), :].reshape(rows // 8 + 1, 8, -1)
    turned = pltpu.roll(tiles, lax.rem(8 - part, 8), 1)
    here = lax.broadcasted_iota(jnp.int32, turned[1:].shape, 1) < 8 - part
    return jnp.where(here, turned[:-1], turned[1:]).reshape(rows, -1)


def detect_kernel(last, place_ref, off_ref, near_ref, out_ref, wide):
    segs, rows, length = wide.shape[0], out_ref.shape[1], out_ref.shape[2]
    t = pl.program_id(0)

    @pl.when(t == 0)
    def _():
        wide[:, DMAX : DMAX + rows] = near_ref[:, DMAX : DMAX + rows]
        for s in range(segs):
            low, up = near_ref[s, :DMAX], near_ref[s, DMAX + rows :]
            wide[s, :DMAX] = jnp.where(place_ref[0] == 0, pltpu.roll(low, 1, 1), low)
            wide[s, DMAX + rows : 2 * DMAX + rows] = jnp.where(
                place_ref[0] == last, pltpu.roll(up, length - 1, 1), up
            )

    batch = out_ref.shape[0]
    for i in range(batch):
        total = shifted(wide, 0, DMAX + off_ref[0, t * batch + i], rows)
        for s in range(1, segs):
            total = total + shifted(wide, s, DMAX + off_ref[s, t * batch + i], rows)
        out_ref[i] = total / segs


def detect(near, offsets):
    segs, rows, length = near.shape
    rows = rows - 2 * DMAX
    place = lax.axis_index("tm").reshape(1)
    templates = offsets.shape[0]
    batch = math.gcd(2, templates)
    smem = pl.BlockSpec(memory_space=pltpu.SMEM)
    return pl.pallas_call(
        functools.partial(detect_kernel, lax.axis_size("tm") - 1),
        grid=(templates // batch,),
        in_specs=[smem, smem, pl.BlockSpec(near.shape, lambda t: (0, 0, 0))],
        out_specs=pl.BlockSpec((batch, rows, length), lambda t: (t, 0, 0)),
        out_shape=jax.ShapeDtypeStruct((templates, rows, length), jnp.float32),
        scratch_shapes=[pltpu.VMEM((segs, rows + 3 * DMAX, length), jnp.float32)],
    )(place, offsets.T, near)


def with_halo(fstat):
    rows = fstat.shape[1]
    count = lax.axis_size("tm")
    up = [(i, (i + 1) % count) for i in range(count)]
    lower = lax.ppermute(fstat[:, rows - DMAX :], "tm", up)
    upper = lax.ppermute(fstat[:, :DMAX], "tm", [(b, a) for a, b in up])
    return jnp.concatenate([lower, fstat, upper], axis=1)


def expand(length, first, thin, real_ref, imag_ref):
    high_real, high_imag, low_real, low_imag = thin
    step = low_real.shape[0]
    for scale, real, imag in ((step, high_real, high_imag), (1, low_real, low_imag)):
        rows = scale * lax.broadcasted_iota(jnp.int32, real.shape, 0)
        columns = first + lax.broadcasted_iota(jnp.int32, real.shape, 1)
        real[...], imag[...] = unit(lax.rem(rows * columns, jnp.full_like(rows, length)), length)

    def body(a, carry):
        real, imag = turned_by(
            high_real[pl.ds(a, 1), :], high_imag[pl.ds(a, 1), :], low_real[...], low_imag[...]
        )
        place = pl.ds(pl.multiple_of(a * step, step), step)
        real_ref[place, :] = real.astype(real_ref.dtype)
        imag_ref[place, :] = imag.astype(imag_ref.dtype)
        return carry

    lax.fori_loop(0, high_real.shape[0], body, 0)


def spectrum_kernel(count, *refs):
    coef, given, out = refs[:3]
    members, twiddled, arrived, wide = refs[3:7]
    turn_real, turn_imag, short_real, short_imag, long_real, long_imag = refs[7:13]
    go_sem, come_sem, back_sem, land_sem, rim_sem, edge_sem = refs[13:19]
    thin_turn, thin_short, thin_long = refs[19:23], refs[23:27], refs[27:31]
    series, field, load_sem = refs[31:]
    segs, comps, part, length = series.shape
    rows, width = members.shape[2:]
    me = lax.axis_index("tm")
    my_rows = pl.ds(pl.multiple_of(me * part, part), part)
    my_columns = pl.ds(pl.multiple_of(me * width, width), width)
    chunks = [(s, lead) for s in range(segs) for lead in range(0, comps, 2)]

    load = pltpu.make_async_copy(given, series, load_sem)
    load.start()
    barrier = pltpu.get_barrier_semaphore()

    def greet(step, carry):
        pl.semaphore_signal(barrier, inc=1, device_id={"tm": lax.rem(me + step, count)})
        return carry

    def to_each(start):
        if count % 2:
            return lax.fori_loop(1, count, lambda n, c: start(lax.rem(me + n, count), c), 0)
        mid = count // 2
        side, seat = me // mid, lax.rem(me, mid)

        def body(n, carry):
            turn = lax.rem(seat + n, mid)
            start(side * mid + turn, carry)
            return start((1 - side) * mid + turn, carry)

        start((1 - side) * mid + seat, 0)
        return lax.fori_loop(1, mid, body, 0)

    lax.fori_loop(1, count, greet, 0)
    pl.semaphore_wait(barrier, count - 1)
    load.wait()

    for q, (s, lead) in enumerate(chunks):
        pair = pl.ds(lead, 2)

        def send(peer, carry):
            theirs = pl.ds(pl.multiple_of(peer * width, width), width)
            pltpu.make_async_remote_copy(
                src_ref=series.at[s, pair, :, theirs],
                dst_ref=members.at[s, pair, my_rows, :],
                send_sem=go_sem.at[q],
                recv_sem=come_sem.at[q],
                device_id={"tm": peer},
            ).start()
            return carry

        to_each(send)

    for s in range(segs):
        for c in range(comps):
            members[s, c, my_rows, :] = series[s, c, :, my_columns]
    expand(rows * length, me * width, thin_turn, turn_real, turn_imag)
    expand(rows, 0, thin_short, short_real, short_imag)

    def settle(sem, q):
        some = members.at[0, pl.ds(0, 2), pl.ds(0, (count - 1) * part), :]
        pltpu.make_async_copy(some, some, sem.at[q]).wait()

    tile = math.gcd(256, rows)
    for q, (s, lead) in enumerate(chunks):
        settle(come_sem, q)
        pair = pl.ds(lead, 2)
        both = jnp.concatenate([members[s, lead], members[s, lead + 1]], axis=-1)

        def strip(r, carry):
            place = pl.ds(pl.multiple_of(r * tile, tile), tile)
            by_real = dot(short_real[place, :], both)
            by_imag = dot(short_imag[place, :], both)
            real, imag = turned_by(
                by_real[:, :width] - by_imag[:, width:],
                by_imag[:, :width] + by_real[:, width:],
                turn_real[place, :],
                turn_imag[place, :],
            )
            twiddled[s, lead, place, :] = real.astype(jnp.bfloat16)
            twiddled[s, lead + 1, place, :] = imag.astype(jnp.bfloat16)
            return carry

        lax.fori_loop(0, rows // tile, strip, 0)

        def send_back(peer, carry):
            theirs = pl.ds(pl.multiple_of(peer * part, part), part)
            pltpu.make_async_remote_copy(
                src_ref=twiddled.at[s, pair, theirs, :],
                dst_ref=arrived.at[s, pair, :, my_columns],
                send_sem=back_sem.at[q],
                recv_sem=land_sem.at[q],
                device_id={"tm": peer},
            ).start()
            return carry

        to_each(send_back)
        for c in (lead, lead + 1):
            arrived[s, c, :, my_columns] = twiddled[s, c, my_rows, :]
        if q == 0:
            expand(length, 0, thin_long, long_real, long_imag)

    slab = math.gcd(512, length)
    rims = []
    last = comps - 2
    for q, (s, lead) in enumerate(chunks):
        settle(land_sem, q)
        a, b, c = coef[s, 0], coef[s, 1], coef[s, 2]

        def project(k, carry):
            place = pl.ds(pl.multiple_of(k * slab, slab), slab)
            flat = arrived[s, lead : lead + 2].reshape(2 * part, length)
            by_real = dot(flat, long_real[:, place])
            by_imag = dot(flat, long_imag[:, place])
            real, imag = by_real[:part] - by_imag[part:], by_imag[:part] + by_real[part:]
            if lead != last:
                field[0, :, place] = real
                field[1, :, place] = imag
                return carry
            ar, ai, br, bi = field[0, :, place], field[1, :, place], real, imag
            numer = (
                b * (ar * ar + ai * ai) + a * (br * br + bi * bi) - 2.0 * c * (ar * br + ai * bi)
            )
            scale = (a * b - c * c) * float(rows * length)
            wide[s, DMAX : DMAX + part, place] = numer / scale
            return carry

        lax.fori_loop(0, length // slab, project, 0, unroll=2)
        if lead != last:
            continue
        for way, (source, target, peer) in enumerate(
            [
                (part, 0, lax.rem(me + 1, count)),
                (DMAX, DMAX + part, lax.rem(me + count - 1, count)),
            ]
        ):
            rim = pltpu.make_async_remote_copy(
                src_ref=wide.at[s, pl.ds(source, DMAX), :],
                dst_ref=wide.at[s, pl.ds(target, DMAX), :],
                send_sem=rim_sem.at[s, way],
                recv_sem=edge_sem.at[s, way],
                device_id={"tm": peer},
            )
            rim.start()
            rims.append(rim)
    for q in range(len(chunks)):
        settle(go_sem, q)
        settle(back_sem, q)
    own = slice(DMAX, DMAX + part)
    out[:, own] = wide[:, own]
    for rim in rims:
        rim.wait()
    out[:, :DMAX] = wide[:, :DMAX]
    out[:, DMAX + part :] = wide[:, DMAX + part :]


def spectrum(series, antenna, count):
    segs, comps, part, length = series.shape
    rows, width = part * count, length // count
    vmem = pl.BlockSpec(memory_space=pltpu.VMEM)
    half = jnp.bfloat16

    def thin(tall, across):
        return [pltpu.VMEM((n, across), jnp.float32) for n in (tall // 32, tall // 32, 32, 32)]

    chunks = segs * comps // 2
    dma = pltpu.SemaphoreType.DMA
    near = (segs, part + 2 * DMAX, length)
    return pl.pallas_call(
        functools.partial(spectrum_kernel, count),
        in_specs=[pl.BlockSpec(memory_space=pltpu.SMEM), pl.BlockSpec(memory_space=pl.ANY)],
        out_specs=vmem,
        out_shape=jax.ShapeDtypeStruct(near, jnp.float32),
        scratch_shapes=[
            pltpu.VMEM((segs, comps, rows, width), half),
            pltpu.VMEM((segs, comps, rows, width), half),
            pltpu.VMEM(series.shape, half),
            pltpu.VMEM(near, jnp.float32),
            pltpu.VMEM((rows, width), jnp.float32),
            pltpu.VMEM((rows, width), jnp.float32),
            pltpu.VMEM((rows, rows), half),
            pltpu.VMEM((rows, rows), half),
            pltpu.VMEM((length, length), half),
            pltpu.VMEM((length, length), half),
            dma((chunks,)),
            dma((chunks,)),
            dma((chunks,)),
            dma((chunks,)),
            dma((segs, 2)),
            dma((segs, 2)),
        ]
        + thin(rows, width)
        + thin(rows, rows)
        + thin(length, length)
        + [
            pltpu.VMEM(series.shape, half),
            pltpu.VMEM((2, part, length), jnp.float32),
            dma,
        ],
        compiler_params=pltpu.CompilerParams(
            collective_id=0, has_side_effects=True, vmem_limit_bytes=60 * 1024 * 1024
        ),
    )(antenna, series)


def local(series, antenna, offsets):
    count = lax.axis_size("tm")
    rows, length = series.shape[2] * count, series.shape[3]
    width = length // count
    if width % 128 == 0 and series.shape[2] % 32 == 0:
        return detect(spectrum(series, antenna, count), offsets)
    bins = rows * length
    columns = lax.axis_index("tm") * width + jnp.arange(width, dtype=jnp.int32)
    turns = jnp.arange(rows, dtype=jnp.int32)[:, None] * columns[None, :] % bins
    twiddle = unit(turns, bins)
    short, long = dft_table(rows), dft_table(length)
    members = lax.all_to_all(series, "tm", split_axis=3, concat_axis=2, tiled=True)
    twiddled = first_stage(members, short, twiddle)
    members = lax.all_to_all(twiddled, "tm", split_axis=2, concat_axis=3, tiled=True)
    fstat = second_stage(members, long, antenna, bins)
    return detect(with_halo(fstat), offsets)


def solution(mesh):
    return jax.shard_map(
        local,
        mesh=mesh,
        in_specs=(P("sky", None, "tm", None), P("sky", None), P("sky", None)),
        out_specs=P("sky", "tm", None),
        check_vma=False,
    )
```
